128 devices in a mesh: row: 8 (over z, x_lo), col: 16 (over x_hi, y, core).
Axes of the slice: x: 4 (x_hi: 2, x_lo: 2; x = x_hi * 2 + x_lo), y: 4, z: 4, core: 2. Of those that a mesh axis runs over, the one named last changes fastest.
Arguments:
- tokens: bfloat16 [8192, 2048], P(('row', 'col')), may hold values from -6 to 6
- timestep: int32 [1], replicated, may hold values from 0 to 999
- mod_weight: float32 [256, 2048], replicated, may hold values from -0.375 to 0.375
- qkv_weight: bfloat16 [3, 2048, 2048], P(None, None, 'col'), may hold values from -0.125 to 0.125
- attn_scale: float32 [16], P('col'), may hold values from 4 to 40
- out_weight: bfloat16 [2048, 2048], P('col'), may hold values from -0.5 to 0.5
- grad_update: bfloat16 [8192, 2048], P(('row', 'col')), may hold values from -6 to 6
Outputs:
- update: bfloat16 [8192, 2048], P(('row', 'col'))
- grad_tokens: bfloat16 [8192, 2048], P(('row', 'col'))
- grad_qkv: float32 [3, 2048, 2048], P(None, 'row', 'col')
- grad_out: float32 [2048, 2048], P('col', 'row')
The draws below stay inside these ranges and needn't reach their ends.
All inputs are finite; a program needn't handle non-finite values.
Results may differ from the reference program's by a relative error of at most 0.018.
Values may be sent and summed in bfloat16 or wider, within the bound.
No kernel may reach another device: no remote copies, remote signals or barrier semaphores. Data moves between devices by JAX's collectives and lax.ppermute only.
A program may use at most 128 MiB of HBM per device.

```python
import math
import jax
import jax.numpy as jnp
from jax import lax

D = 2048
HEADS = 16
FREQS = 128
HDIM = 128
TOKENS = 8192


def block_levels(key, shape, pieces, least, high):
    def one(position, parts):
        draws = jax.random.uniform(jax.random.fold_in(jax.random.fold_in(key, 6), position), (parts,), jnp.float32, least / len(pieces), high / len(pieces))
        return jnp.repeat(jnp.exp(draws), shape[position] // parts).reshape((-1,) + (1,) * (len(shape) - position - 1))

    loudness = one(*pieces[0])
    for cut in pieces[1:]:
        loudness = loudness * one(*cut)
    return loudness


def centred(stream_key, shape, scale, bound, split=(), held_as=jnp.bfloat16):
    entries = jax.random.normal(stream_key, shape, jnp.float32) * scale
    if len(split) > 0:
        entries = block_levels(stream_key, shape, split, -0.22, 0.18) * entries
    return jnp.clip(entries, min=-bound, max=bound).astype(held_as)


def setup_inputs(seed: int = 0) -> dict:
    streams_of = jax.random.split(jax.random.key(seed), 8)
    tokens = centred(streams_of[0], (TOKENS, D), 1.0, 6.0, ((0, 128),))
    timestep = jax.random.randint(streams_of[1], (1,), 0, 1000).astype(jnp.int32)
    mod_weight = centred(streams_of[2], (2 * FREQS, D), (2 * FREQS) ** -0.5, 0.375, (), jnp.float32)
    qkv_weight = centred(streams_of[3], (3, D, D), D ** -0.5, 0.125, ((2, 16),))
    attn_scale = jnp.clip(jnp.exp(math.log(40.0) - 2.3025851 * jax.random.uniform(streams_of[4], (HEADS,), jnp.float32) ** block_levels(streams_of[4], (HEADS,), ((0, 16),), -0.2, 0.2)), 4.0, 40.0)
    out_weight = centred(streams_of[5], (D, D), HDIM ** -0.5, 0.5, ((0, 16),))
    grad_update = centred(streams_of[6], (TOKENS, D), 1.0, 6.0, ((0, 128),))
    return dict(tokens=tokens, timestep=timestep, mod_weight=mod_weight, qkv_weight=qkv_weight, attn_scale=attn_scale, out_weight=out_weight, grad_update=grad_update)


epsilon = 1e-06

def embed(timestep, count):
    index = jnp.arange(count, dtype=jnp.float32)
    freqs = jnp.exp(-math.log(10000.0) * index / count)
    angles = timestep.astype(jnp.float32)[0] * freqs
    return jnp.concatenate([jnp.cos(angles), jnp.sin(angles)])

def unit_rows(values):
    factor = lax.rsqrt(lax.optimization_barrier(jnp.mean(values * values, -1, keepdims=True)) + epsilon)
    return (values * factor, factor)

def unit_grad(grad_unit, unit, factor):
    return factor * (grad_unit - unit * lax.optimization_barrier(jnp.mean(grad_unit * unit, -1, keepdims=True)))

def forward_head(packed):
    query, key_rows, value_rows, scale = packed
    head_dim = query.shape[1]
    coeff = scale / head_dim
    size = math.gcd(query.shape[0], 512)
    blocks = query.reshape(query.shape[0] // size, size, head_dim)

    def one_block(query_block):
        scores = jnp.dot(query_block, key_rows.T, preferred_element_type=jnp.float32) * coeff
        weights = jnp.exp(scores - scale)
        totals = lax.optimization_barrier(jnp.sum(weights, -1))
        mixed = jnp.dot(weights.astype(jnp.bfloat16), value_rows, preferred_element_type=jnp.float32)
        return (totals, mixed)
    totals, mixed = lax.map(one_block, blocks)
    return (totals.reshape(-1), mixed.reshape(-1, head_dim))

def backward_head(packed):
    query, key_rows, value_rows, grad_rows, delta_rows, inverse_rows, scale = packed
    head_dim = query.shape[1]
    coeff = scale / head_dim
    length = query.shape[0]
    size = math.gcd(length, 512)
    blocks = (query.reshape(length // size, size, head_dim), grad_rows.reshape(length // size, size, head_dim), delta_rows.reshape(length // size, size), inverse_rows.reshape(length // size, size))

    def step(state, block):
        query_block, grad_block, delta_block, inverse_block = block
        scores = jnp.dot(query_block, key_rows.T, preferred_element_type=jnp.float32) * coeff
        probs = jnp.exp(scores - scale) * inverse_block[:, None]
        dprobs = jnp.dot(grad_block, value_rows.T, preferred_element_type=jnp.float32)
        dscores = (probs * (dprobs - delta_block[:, None]) * coeff).astype(jnp.bfloat16)
        grad_query = jnp.dot(dscores, key_rows, preferred_element_type=jnp.float32)
        grad_key = state[0] + jnp.dot(dscores.T, query_block, preferred_element_type=jnp.float32)
        grad_value = state[1] + jnp.dot(probs.astype(jnp.bfloat16).T, grad_block, preferred_element_type=jnp.float32)
        return ((grad_key, grad_value), grad_query)
    empty = jnp.zeros((length, head_dim), jnp.float32)
    (grad_key, grad_value), grad_query = lax.scan(step, (empty, empty), blocks)
    return (grad_query.reshape(length, head_dim), grad_key, grad_value)

def reference(tokens, timestep, mod_weight, qkv_weight, attn_scale, out_weight, grad_update):
    length, width = tokens.shape
    heads = attn_scale.shape[0]
    head_dim = width // heads
    embedded = embed(timestep, mod_weight.shape[0] // 2)
    gain = 1.0 + lax.optimization_barrier(jnp.sum(embedded[:, None] * mod_weight, 0))
    tok_float = tokens.astype(jnp.float32)
    rstd = lax.rsqrt(lax.optimization_barrier(jnp.mean(tok_float * tok_float, -1, keepdims=True)) + epsilon)
    normed = tok_float * rstd
    hidden = (normed * gain).astype(jnp.bfloat16)
    raw = jnp.stack([jnp.dot(hidden, qkv_weight[k], preferred_element_type=jnp.float32) for k in range(3)])
    query_unit, query_factor = unit_rows(raw[0].reshape(length, heads, head_dim))
    key_unit, key_factor = unit_rows(raw[1].reshape(length, heads, head_dim))
    query_heads = jnp.transpose(query_unit.astype(jnp.bfloat16), (1, 0, 2))
    key_heads = jnp.transpose(key_unit.astype(jnp.bfloat16), (1, 0, 2))
    value_heads = jnp.transpose(raw[2].astype(jnp.bfloat16).reshape(length, heads, head_dim), (1, 0, 2))
    totals, mixed = lax.map(forward_head, (query_heads, key_heads, value_heads, attn_scale))
    attended_heads = (mixed / totals[:, :, None]).astype(jnp.bfloat16)
    attended = jnp.transpose(attended_heads, (1, 0, 2)).reshape(length, width)
    update = jnp.dot(attended, out_weight, preferred_element_type=jnp.float32).astype(jnp.bfloat16)
    grad_out = jnp.dot(attended.T, grad_update, preferred_element_type=jnp.float32)
    grad_attended = jnp.dot(grad_update, out_weight.T, preferred_element_type=jnp.float32).astype(jnp.bfloat16)
    grad_heads = jnp.transpose(grad_attended.reshape(length, heads, head_dim), (1, 0, 2))
    delta = lax.optimization_barrier(jnp.sum(grad_heads.astype(jnp.float32) * attended_heads.astype(jnp.float32), -1))
    inverse = 1.0 / totals
    grad_query, grad_key, grad_value = lax.map(backward_head, (query_heads, key_heads, value_heads, grad_heads, delta, inverse, attn_scale))
    grad_query = jnp.transpose(grad_query, (1, 0, 2))
    grad_key = jnp.transpose(grad_key, (1, 0, 2))
    grad_value = jnp.transpose(grad_value, (1, 0, 2))
    grad_q = unit_grad(grad_query, query_unit, query_factor).astype(jnp.bfloat16).reshape(length, width)
    grad_k = unit_grad(grad_key, key_unit, key_factor).astype(jnp.bfloat16).reshape(length, width)
    grad_v = grad_value.astype(jnp.bfloat16).reshape(length, width)
    grad_raw = [grad_q, grad_k, grad_v]
    grad_qkv = jnp.stack([jnp.dot(hidden.T, grad_raw[k], preferred_element_type=jnp.float32) for k in range(3)])
    grad_hidden = jnp.dot(grad_raw[0], qkv_weight[0].T, preferred_element_type=jnp.float32)
    grad_hidden = grad_hidden + jnp.dot(grad_raw[1], qkv_weight[1].T, preferred_element_type=jnp.float32)
    grad_hidden = grad_hidden + jnp.dot(grad_raw[2], qkv_weight[2].T, preferred_element_type=jnp.float32)
    grad_normed = grad_hidden * gain
    grad_tokens = (rstd * (grad_normed - normed * lax.optimization_barrier(jnp.mean(grad_normed * normed, -1, keepdims=True)))).astype(jnp.bfloat16)
    return (update, grad_tokens, grad_qkv, grad_out)
```

```python
import functools
import math

import jax
import jax.numpy as jnp
from jax import lax
from jax.experimental import pallas as pl
from jax.experimental.pallas import tpu as pltpu
from jax.sharding import PartitionSpec as P


epsilon = 1e-06
F = jnp.float32
B = jnp.bfloat16
NT = (((1,), (1,)), ((), ()))
NN = (((1,), (0,)), ((), ()))
TN = (((0,), (0,)), ((), ()))


def dot(a, b, dims=NN):
    return lax.dot_general(a, b, dims, preferred_element_type=F)


def col_move(x, xhi=0, y=0, core=0):
    perm = []
    for h in range(2):
        for w in range(4):
            for k in range(2):
                perm.append((h * 8 + w * 2 + k, (h ^ xhi) * 8 + (w + y) % 4 * 2 + (k ^ core)))
    return lax.ppermute(x, "col", perm)


def row_move(x, z=0, xlo=0):
    perm = []
    for w in range(4):
        for k in range(2):
            perm.append((w * 2 + k, (w + z) % 4 * 2 + (k ^ xlo)))
    return lax.ppermute(x, "row", perm)


def after(x, *deps):
    return lax.optimization_barrier((x,) + deps)[0]


def gather_col(own):
    across = col_move(own, xhi=1)
    base = jnp.concatenate([own, across], 0)
    slots = [base] + [col_move(base, y=d) for d in (1, 3, 2)]
    return slots + [col_move(slot, core=1) for slot in slots]


def scatter_col(part):
    there = col_move(part(1), core=1)
    total = part(0).astype(F) + there.astype(F)
    rows = total.shape[0] // 4
    kept = total[:rows]
    for slot, d in enumerate((1, 3, 2)):
        sent = total[(slot + 1) * rows : (slot + 2) * rows].astype(B)
        kept = kept + col_move(sent, y=-d).astype(F)
    there = col_move(kept[rows // 2 :].astype(B), xhi=1)
    return kept[: rows // 2] + there.astype(F)


def qkv_kernel(w_ref, *rest):
    slots, (q_out, kv_out, raw_out, rows, weight, sems) = rest[:8], rest[8:]
    copies = [
        pltpu.make_async_copy(slot, rows.at[pl.ds(n * 128, 128)], sems.at[n])
        for n, slot in enumerate(slots)
    ]
    for copy in copies:
        copy.start()
    for k in range(3):
        weight[:, k * 128 : (k + 1) * 128] = w_ref[k]
    for copy in copies:
        copy.wait()

    @pl.loop(0, 4)
    def _(n):
        at = pl.ds(pl.multiple_of(n * 256, 256), 256)
        raw = dot(rows[at, :], weight[...])
        query, key = unit_rows(raw[:, :128])[0], unit_rows(raw[:, 128:256])[0]
        q_out[at, :] = query.astype(B)
        kv_out[at, 0:128] = key.astype(B)
        kv_out[at, 128:256] = raw[:, 256:].astype(B)
        raw_out[at, :] = raw[:, :256]


def project(weight, slots):
    any_space = pl.BlockSpec(memory_space=pl.ANY)
    rows = 8 * slots[0].shape[0]
    width = slots[0].shape[1]
    return pl.pallas_call(
        qkv_kernel,
        in_specs=[pl.BlockSpec(memory_space=pltpu.VMEM)] + [any_space] * 8,
        out_shape=[
            jax.ShapeDtypeStruct((rows, 128), B),
            jax.ShapeDtypeStruct((rows, 256), B),
            jax.ShapeDtypeStruct((rows, 256), F),
        ],
        scratch_shapes=[
            pltpu.VMEM((rows, width), B),
            pltpu.VMEM((width, 384), B),
            pltpu.SemaphoreType.DMA((8,)),
        ],
        name="project",
        cost_estimate=pl.CostEstimate(
            flops=2 * rows * width * 384, bytes_accessed=6 * 1024 * 1024, transcendentals=0
        ),
    )(weight, *slots)


def cotangent_kernel(w_ref, *rest):
    slots, out_ref = rest[:8], rest[8]
    for n, slot in enumerate(slots):
        out_ref[n * 128 : (n + 1) * 128, :] = dot(slot[...], w_ref[...], NT).astype(B)


def project_cotangent(weight, slots):
    rows = 8 * slots[0].shape[0]
    return pl.pallas_call(
        cotangent_kernel,
        in_specs=[pl.BlockSpec(memory_space=pltpu.VMEM)] * 9,
        out_shape=jax.ShapeDtypeStruct((rows, 128), B),
        name="project_cotangent",
        cost_estimate=pl.CostEstimate(
            flops=2 * rows * 2048 * 128, bytes_accessed=5 * 1024 * 1024, transcendentals=0
        ),
    )(weight, *slots)


def weight_grad_kernel(left_ref, att_ref, *rest):
    slots, grads, out_ref = rest[:8], rest[8:16], rest[16]
    cols = jnp.concatenate([slot[...] for slot in slots], 0)
    out_ref[0, 0:384, :] = dot(left_ref[...], cols).astype(B)
    cols = jnp.concatenate([slot[...] for slot in grads], 0)
    out_ref[0, 384:512, :] = dot(att_ref[...], cols).astype(B)


def weight_grads(left, att, slots, grads):
    cut = pl.BlockSpec((128, 256), lambda i: (0, i))
    rows = left.shape[1]
    return pl.pallas_call(
        weight_grad_kernel,
        grid=(8,),
        in_specs=[
            pl.BlockSpec((384, rows), lambda i: (0, 0)),
            pl.BlockSpec((128, rows), lambda i: (0, 0)),
        ]
        + [cut] * 16,
        out_specs=pl.BlockSpec((1, 512, 256), lambda i: (i, 0, 0)),
        out_shape=jax.ShapeDtypeStruct((8, 512, 256), B),
        name="weight_grads",
        cost_estimate=pl.CostEstimate(
            flops=2 * rows * 2048 * 512, bytes_accessed=10 * 1024 * 1024, transcendentals=0
        ),
    )(left, att, *slots, *grads)


def forward_kernel(first, step, count, c_ref, q_ref, *rest):
    kvs, rest = rest[:count], rest[count:]
    acc_in, tot_in, acc, tot = ((None, None) + rest) if first else rest
    c2 = c_ref[0, 0]
    if first:
        acc[...] = jnp.zeros_like(acc)
        tot[...] = jnp.zeros_like(tot)
    else:
        acc[...] = acc_in[...]
        tot[...] = tot_in[...]
    for kv_ref in kvs:

        @pl.loop(0, kv_ref.shape[0] // step)
        def _(j):
            at = pl.ds(pl.multiple_of(j * step, step), step)
            w = jnp.exp2(dot(q_ref[...], kv_ref[at, 0:128], NT) * c2)
            part = w[:, 0:128]
            for g in range(1, step // 128):
                part = part + w[:, g * 128 : (g + 1) * 128]
            tot[...] += part
            acc[...] += dot(w.astype(B), kv_ref[at, 128:256])


def forward_block(c2, q, kvs, state=None, step=512):
    count, keys = q.shape[0], kvs[0].shape[0]
    first = state is None
    vmem = pl.BlockSpec(memory_space=pltpu.VMEM)
    args = [c2, q, *kvs] + ([] if first else list(state))
    return pl.pallas_call(
        functools.partial(forward_kernel, first, step, len(kvs)),
        in_specs=[pl.BlockSpec(memory_space=pltpu.SMEM)] + [vmem] * (len(args) - 1),
        out_specs=[vmem] * 2,
        out_shape=[jax.ShapeDtypeStruct((count, 128), F)] * 2,
        name="forward_block",
        cost_estimate=pl.CostEstimate(
            flops=4 * len(kvs) * count * keys * 128,
            bytes_accessed=count * 2048,
            transcendentals=len(kvs) * count * keys,
        ),
    )(*args)


def backward_kernel(first, step, c_ref, q_ref, qs_ref, do_ref, dos_ref, dl_ref, kv_ref, *rest):
    dq_in, dq, dkv_out, dk, dv = ((None,) + rest) if first else rest
    i = pl.program_id(0)
    c2 = c_ref[0, 0]

    @pl.when(i == 0)
    def _():
        dk[...] = jnp.zeros_like(dk)
        dv[...] = jnp.zeros_like(dv)

    if first:
        dq[...] = jnp.zeros_like(dq)
    else:
        dq[...] = dq_in[...]

    @pl.loop(0, kv_ref.shape[0] // step)
    def _(j):
        at = pl.ds(pl.multiple_of(j * step, step), step)
        k = kv_ref[at, 0:128]
        w = jnp.exp2(dot(k, q_ref[...], NT) * c2)
        t = (w * (dot(kv_ref[at, 128:256], do_ref[...], NT) - dl_ref[...])).astype(B)
        dv[at, :] += dot(w.astype(B), dos_ref[...])
        dk[at, :] += dot(t, qs_ref[...])
        dq[...] += dot(t, k, TN)

    @pl.when(i == pl.num_programs(0) - 1)
    def _():
        dkv_out[:, 0:128] = dk[...].astype(dkv_out.dtype)
        dkv_out[:, 128:256] = dv[...].astype(dkv_out.dtype)


def backward_block(c2, rows, delta, kv, state, out, block=1024, step=512):
    count, keys = rows[0].shape[0], kv.shape[0]
    first = state is None
    row = pl.BlockSpec((block, 128), lambda i: (i, 0))
    full = pl.BlockSpec((keys, 256), lambda i: (0, 0))
    specs = [pl.BlockSpec(memory_space=pltpu.SMEM), row, row, row, row]
    specs += [pl.BlockSpec((1, block), lambda i: (0, i)), full]
    args = [c2, *rows, delta, kv]
    if not first:
        specs += [row]
        args += [state]
    return pl.pallas_call(
        functools.partial(backward_kernel, first, step),
        grid=(count // block,),
        in_specs=specs,
        out_specs=[row, full],
        out_shape=[jax.ShapeDtypeStruct((count, 128), F), jax.ShapeDtypeStruct((keys, 256), out)],
        scratch_shapes=[pltpu.VMEM((keys, 128), F)] * 2,
        name="backward_block",
        cost_estimate=pl.CostEstimate(
            flops=10 * count * keys * 128, bytes_accessed=count * 3072, transcendentals=count * keys
        ),
    )(*args)


def embed(timestep, count):
    index = jnp.arange(count, dtype=F)
    freqs = jnp.exp(-math.log(10000.0) * index / count)
    angles = timestep.astype(F)[0] * freqs
    return jnp.concatenate([jnp.cos(angles), jnp.sin(angles)])


def unit_rows(values):
    factor = lax.rsqrt(jnp.mean(values * values, -1, keepdims=True) + epsilon)
    return (values * factor, factor)


def unit_grad(grad_unit, unit, factor):
    return factor * (grad_unit - unit * jnp.mean(grad_unit * unit, -1, keepdims=True))


def layer(tokens, timestep, mod_weight, qkv_weight, attn_scale, out_weight, grad_update):
    coeff = attn_scale[0] / 128
    c2 = (coeff * (1.0 / math.log(2.0))).reshape(1, 1)
    embedded = embed(timestep, mod_weight.shape[0] // 2)
    gain = 1.0 + jnp.sum(embedded[:, None] * mod_weight, 0)
    tok_float = tokens.astype(F)
    rstd = lax.rsqrt(jnp.mean(tok_float * tok_float, -1, keepdims=True) + epsilon)
    normed = tok_float * rstd
    hidden = (normed * gain).astype(B)

    slots = gather_col(hidden)
    own_q, own_kv, raw = project(qkv_weight, slots)
    count = own_q.shape[0]
    chunk = {0: own_kv}
    for d in (2, 1, 3):
        chunk[d] = row_move(own_kv, z=d)
    q = jnp.concatenate([own_q, row_move(own_q, xlo=1)], 0)

    grads = gather_col(after(grad_update, own_q))
    own_do = project_cotangent(out_weight, grads)
    do = jnp.concatenate([own_do, row_move(own_do, xlo=1)], 0)

    state = forward_block(c2, q, [chunk[0]])
    state = forward_block(c2, q, [chunk[1], chunk[3]], state)
    acc, tot = forward_block(c2, q, [chunk[2]], state)
    sums = jnp.sum(tot, -1)
    there = row_move(acc[count:].astype(B), xlo=1)
    there_sums = row_move(sums[count:].reshape(8, 128), xlo=1).reshape(count)
    mixed = acc[:count] + there.astype(F)
    totals = sums[:count] + there_sums
    inverse = 1.0 / totals
    attended = (mixed / totals[:, None]).astype(B)
    delta = jnp.sum(own_do.astype(F) * attended.astype(F), -1)
    stats = jnp.stack([inverse, delta])
    stats = jnp.concatenate([stats, row_move(stats, xlo=1)], 1)
    inv_col = stats[0][:, None]
    scaled_q = (q.astype(F) * (inv_col * coeff)).astype(B)
    scaled_do = (do.astype(F) * inv_col).astype(B)

    dq = None
    back = {}
    for d in (2, 1, 3, 0):
        dq, dkv = backward_block(
            c2, (q, scaled_q, do, scaled_do), stats[1:2], chunk[d], dq, B if d else F
        )
        if d == 2:
            half = count // 2
            ready = after(attended, dkv)
            update = scatter_col(
                lambda k: dot(ready[k * half : (k + 1) * half], out_weight).astype(B)
            ).astype(B)
        back[d] = row_move(dkv, z=-d).astype(F) if d else dkv
    dkv = back[0] + back[1] + back[2] + back[3]
    there = row_move(dq[count:].astype(B), xlo=1)
    dq = (dq[:count] + there.astype(F)) * (inverse * coeff)[:, None]
    grad_q = unit_grad(dq, *unit_rows(raw[:, :128])).astype(B)
    grad_k = unit_grad(dkv[:, :128], *unit_rows(raw[:, 128:256])).astype(B)
    grad_raw = jnp.concatenate([grad_q, grad_k, dkv[:, 128:].astype(B)], 1)

    weight = jnp.concatenate([qkv_weight[0], qkv_weight[1], qkv_weight[2]], 1)
    grad_hidden = scatter_col(
        lambda k: dot(grad_raw[k * half : (k + 1) * half], weight, NT).astype(B)
    )
    part = weight_grads(grad_raw.T, attended.T, slots, grads)
    part = lax.all_to_all(part, "row", 0, 0, tiled=True)
    total = jnp.sum(part.astype(F), 0)
    grad_qkv = jnp.transpose(total[:384].reshape(3, 128, 256), (0, 2, 1))
    grad_normed = grad_hidden * gain
    grad_tokens = (
        rstd * (grad_normed - normed * jnp.mean(grad_normed * normed, -1, keepdims=True))
    ).astype(B)
    return (update, grad_tokens, grad_qkv, total[384:])


def solution(mesh):
    placed = (
        P(("row", "col"), None),
        P(),
        P(),
        P(None, None, "col"),
        P("col"),
        P("col", None),
        P(("row", "col"), None),
    )
    return jax.shard_map(
        layer,
        mesh=mesh,
        in_specs=placed,
        out_specs=(
            P(("row", "col"), None),
            P(("row", "col"), None),
            P(None, "row", "col"),
            P("col", "row"),
        ),
        check_vma=False,
    )
```

```python
import functools
import math

import jax
import jax.numpy as jnp
from jax import lax
from jax.experimental import pallas as pl
from jax.experimental.pallas import tpu as pltpu
from jax.sharding import PartitionSpec as P


epsilon = 1e-06
F = jnp.float32
B = jnp.bfloat16
NT = (((1,), (1,)), ((), ()))
NN = (((1,), (0,)), ((), ()))
TN = (((0,), (0,)), ((), ()))


def dot(a, b, dims=NN):
    return lax.dot_general(a, b, dims, preferred_element_type=F)


def col_move(x, xhi=0, y=0, core=0):
    perm = []
    for h in range(2):
        for w in range(4):
            for k in range(2):
                perm.append((h * 8 + w * 2 + k, (h ^ xhi) * 8 + (w + y) % 4 * 2 + (k ^ core)))
    return lax.ppermute(x, "col", perm)


def row_move(x, z=0, xlo=0):
    perm = []
    for w in range(4):
        for k in range(2):
            perm.append((w * 2 + k, (w + z) % 4 * 2 + (k ^ xlo)))
    return lax.ppermute(x, "row", perm)


def after(x, *deps):
    return lax.optimization_barrier((x,) + deps)[0]


TURNS = (1, 3, 2)


def with_core(slots):
    pairs = [(slot, col_move(slot, core=1)) for slot in slots]
    return [slot for pair in pairs for slot in pair]


def project_kernel(second, w_ref, *rest):
    slots, rest = rest[:8], rest[8:]
    prev, rest = (rest[:2], rest[2:]) if second else ((), rest)
    q_out, kv_out, raw_out, rows, weight, sems = rest
    size = slots[0].shape[0]
    base = prev[0].shape[0] if second else 0
    copies = [
        pltpu.make_async_copy(slot, rows.at[pl.ds(n * size, size)], sems.at[n])
        for n, slot in enumerate(slots)
    ]
    for copy in copies:
        copy.start()
    for k in range(3):
        weight[:, k * 128 : (k + 1) * 128] = w_ref[k]
    if second:
        q_out[0:base, :] = prev[0][...]
        raw_out[0:base, :] = prev[1][...]
    for copy in copies:
        copy.wait()

    @pl.loop(0, 2)
    def _(n):
        raw = dot(rows[pl.ds(pl.multiple_of(n * 256, 256), 256), :], weight[...])
        at = pl.ds(pl.multiple_of(base + n * 256, 256), 256)
        here = pl.ds(pl.multiple_of(n * 256, 256), 256)
        q_out[at, :] = unit_rows(raw[:, :128])[0].astype(B)
        kv_out[here, 0:128] = unit_rows(raw[:, 128:256])[0].astype(B)
        kv_out[here, 128:256] = raw[:, 256:].astype(B)
        raw_out[at, :] = raw[:, :256]


def project(weight, slots, prev=()):
    rows, width = 8 * slots[0].shape[0], slots[0].shape[1]
    total = rows * (2 if prev else 1)
    vmem = pl.BlockSpec(memory_space=pltpu.VMEM)
    return pl.pallas_call(
        functools.partial(project_kernel, bool(prev)),
        in_specs=[vmem] + [pl.BlockSpec(memory_space=pl.ANY)] * 8 + [vmem] * len(prev),
        out_shape=[
            jax.ShapeDtypeStruct((total, 128), B),
            jax.ShapeDtypeStruct((rows, 256), B),
            jax.ShapeDtypeStruct((total, 256), F),
        ],
        scratch_shapes=[
            pltpu.VMEM((rows, width), B),
            pltpu.VMEM((width, 384), B),
            pltpu.SemaphoreType.DMA((8,)),
        ],
        name="project",
        cost_estimate=pl.CostEstimate(
            flops=2 * rows * width * 384, bytes_accessed=6 * 1024 * 1024, transcendentals=0
        ),
    )(weight, *slots, *prev)


def token_copies(slots, rows, sems):
    half = slots[0].shape[0] // 2
    return [
        pltpu.make_async_copy(
            slot.at[pl.ds(h * half, half)], rows.at[pl.ds((h * 8 + n) * half, half)], sems.at[h * 8 + n]
        )
        for h in range(2)
        for n, slot in enumerate(slots)
    ]


def cotangent_kernel(w_ref, *rest):
    slots, (out_ref, rows, sems) = rest[:8], rest[8:]
    copies = token_copies(slots, rows, sems)
    for copy in copies:
        copy.start()
    for copy in copies:
        copy.wait()

    @pl.loop(0, 2)
    def _(n):
        at = pl.ds(pl.multiple_of(n * 512, 512), 512)
        out_ref[at, :] = dot(rows[at, :], w_ref[...], NT).astype(B)


def project_cotangent(weight, slots):
    rows, width = 8 * slots[0].shape[0], slots[0].shape[1]
    vmem = pl.BlockSpec(memory_space=pltpu.VMEM)
    return pl.pallas_call(
        cotangent_kernel,
        in_specs=[vmem] + [pl.BlockSpec(memory_space=pl.ANY)] * 8,
        out_shape=jax.ShapeDtypeStruct((rows, 128), B),
        scratch_shapes=[pltpu.VMEM((rows, width), B), pltpu.SemaphoreType.DMA((16,))],
        name="project_cotangent",
        cost_estimate=pl.CostEstimate(
            flops=2 * rows * width * 128, bytes_accessed=5 * 1024 * 1024, transcendentals=0
        ),
    )(weight, *slots)


def weight_grad_kernel(left_ref, att_ref, *rest):
    parts, slots, (out_ref, rows, cots, sems) = rest[:16], rest[16:24], rest[24:]
    size = parts[0].shape[0]
    first = [
        pltpu.make_async_copy(part, rows.at[pl.ds(n * size, size)], sems.at[16 + n])
        for n, part in enumerate(parts)
    ]
    second = token_copies(slots, cots, sems)
    for copy in first + second:
        copy.start()
    for copy in first:
        copy.wait()

    @pl.loop(0, 8)
    def _(n):
        at = pl.ds(pl.multiple_of(n * 256, 256), 256)
        out_ref[n, 0:384, :] = dot(left_ref[...], rows[:, at]).astype(B)

    for copy in second:
        copy.wait()

    @pl.loop(0, 8)
    def _(n):
        at = pl.ds(pl.multiple_of(n * 256, 256), 256)
        out_ref[n, 384:512, :] = dot(att_ref[...], cots[:, at]).astype(B)


def weight_grads(left, att, parts, slots):
    rows, width = left.shape[1], slots[0].shape[1]
    vmem = pl.BlockSpec(memory_space=pltpu.VMEM)
    return pl.pallas_call(
        weight_grad_kernel,
        in_specs=[vmem] * 2 + [pl.BlockSpec(memory_space=pl.ANY)] * 24,
        out_shape=jax.ShapeDtypeStruct((8, 512, width // 8), B),
        scratch_shapes=[pltpu.VMEM((rows, width), B)] * 2 + [pltpu.SemaphoreType.DMA((32,))],
        name="weight_grads",
        cost_estimate=pl.CostEstimate(
            flops=2 * rows * width * 512, bytes_accessed=11 * 1024 * 1024, transcendentals=0
        ),
    )(left, att, *parts, *slots)


def heads_kernel(count, *rest):
    rows, weights, slots = rest[:count], rest[count : 2 * count], rest[2 * count :]
    left = jnp.concatenate([row[...] for row in rows], 1)
    if len(weights[0].shape) == 3:
        grad = dot(left, jnp.concatenate([w[n] for w in weights for n in range(3)], 1), NT)
    else:
        grad = dot(left, jnp.concatenate([w[...] for w in weights], 0))
    size = grad.shape[0] // 4
    for n, slot in enumerate(slots):
        slot[...] = grad[n * size : (n + 1) * size].astype(slot.dtype)


def over_heads(rows, weights):
    count, width = rows[-1].shape
    if len(weights[0].shape) == 3:
        cut = pl.BlockSpec((3, 512, 128), lambda i: (0, i, 0))
    else:
        cut = pl.BlockSpec((128, 512), lambda i: (0, i))
    slot = pl.BlockSpec((count // 4, 512), lambda i: (0, i))
    return pl.pallas_call(
        functools.partial(heads_kernel, len(rows)),
        grid=(4,),
        in_specs=[pl.BlockSpec((count, width), lambda i: (0, 0))] * len(rows) + [cut] * len(rows),
        out_specs=[slot] * 4,
        out_shape=[jax.ShapeDtypeStruct((count // 4, 2048), F)]
        + [jax.ShapeDtypeStruct((count // 4, 2048), B)] * 3,
        name="over_heads",
        cost_estimate=pl.CostEstimate(
            flops=2 * count * width * 4 * 2048, bytes_accessed=8 * 1024 * 1024, transcendentals=0
        ),
    )(*rows, *weights)


def share_rows(near, near_core, far):
    across = col_move(far, xhi=1)
    rest = [col_move(x, core=1) for x in (near_core, across[across.shape[0] // 2 :])]
    return [near, across] + rest


def share_weight(weight):
    across = col_move(weight, xhi=1)
    return [weight, across, col_move(weight, core=1), col_move(across, core=1)]


def to_owners(slots):
    there = [col_move(slot, y=-d) for slot, d in zip(slots[1:], TURNS)]
    return slots[0] + there[0].astype(F) + there[1].astype(F) + there[2].astype(F)


def by_core(rows, near, near_core, far, at=slice(None)):
    size = rows.shape[0] // 16
    for y in range(4):
        for k in range(2):
            piece = rows[(2 * y + k) * size : (2 * y + k + 1) * size]
            (near_core if k else near)[y * size : (y + 1) * size, at] = piece
            piece = rows[(8 + 2 * y + k) * size : (9 + 2 * y + k) * size]
            far[(4 * k + y) * size : (4 * k + y + 1) * size, at] = piece


def forward_kernel(first, last, step, count, c_ref, q_ref, *rest):
    kvs, rest = rest[:count], rest[count:]
    prev, rest = ((), rest) if first else (rest[:2], rest[2:])
    acc_out, tot_out, acc, tot = rest if last else (None, None) + rest
    c2 = c_ref[0, 0]
    if first:
        acc[...] = jnp.zeros_like(acc)
        tot[...] = jnp.zeros_like(tot)
    else:
        acc[...] = prev[0][...]
        tot[...] = prev[1][...]
    for kv_ref in kvs:

        @pl.loop(0, kv_ref.shape[0] // step)
        def _(j):
            at = pl.ds(pl.multiple_of(j * step, step), step)
            w = jnp.exp2(dot(q_ref[...], kv_ref[at, 0:128], NT) * c2)
            part = w[:, 0:128]
            for g in range(1, step // 128):
                part = part + w[:, g * 128 : (g + 1) * 128]
            tot[...] += part
            acc[...] += dot(w.astype(B), kv_ref[at, 128:256])

    if last:
        acc_out[...] = acc[...].astype(B)
        tot_out[...] = jnp.broadcast_to(jnp.sum(tot[...].T, 0, keepdims=True), tot_out.shape)


def forward_block(c2, q, kvs, state=(), last=False, step=512):
    count, keys = q.shape[0], kvs[0].shape[0]
    vmem = pl.BlockSpec(memory_space=pltpu.VMEM)
    args = [c2, q, *kvs, *state]
    if last:
        out = [jax.ShapeDtypeStruct((count, 128), B), jax.ShapeDtypeStruct((8, count), F)]
        scratch = [pltpu.VMEM((count, 128), F)] * 2
    else:
        out = [jax.ShapeDtypeStruct((count, 128), F)] * 2
        scratch = []
    return pl.pallas_call(
        functools.partial(forward_kernel, not state, last, step, len(kvs)),
        in_specs=[pl.BlockSpec(memory_space=pltpu.SMEM)] + [vmem] * (len(args) - 1),
        out_specs=[vmem] * 2,
        out_shape=out,
        scratch_shapes=scratch,
        name="forward_block",
        cost_estimate=pl.CostEstimate(
            flops=4 * len(kvs) * count * keys * 128,
            bytes_accessed=count * 2048,
            transcendentals=len(kvs) * count * keys,
        ),
    )(*args)


def attended_kernel(acc_ref, tot_ref, there_ref, there_tot_ref, do_ref, *rest):
    near, near_core, far, flat_out, stat_out = rest
    total = jnp.sum(tot_ref[...].T, 0, keepdims=True) + there_tot_ref[0:1, :]
    divisor = jnp.broadcast_to(total, (128, total.shape[1])).T
    attended = ((acc_ref[...] + there_ref[...].astype(F)) / divisor).astype(B)
    wide = attended.astype(F)
    delta = jnp.sum((do_ref[...].astype(F) * wide).T, 0, keepdims=True)
    flat_out[...] = wide.T.astype(B)
    by_core(attended, near, near_core, far)
    stat_out[0:1, :] = jnp.log2(total)
    stat_out[1:2, :] = delta
    stat_out[2:8, :] = jnp.zeros((6, total.shape[1]), F)


def finish_attended(acc, tot, there, there_tot, do):
    count = acc.shape[0]
    return pl.pallas_call(
        attended_kernel,
        out_shape=[jax.ShapeDtypeStruct((count // n, 128), B) for n in (4, 4, 2)]
        + [jax.ShapeDtypeStruct((128, count), B), jax.ShapeDtypeStruct((8, count), F)],
        name="finish_attended",
    )(acc, tot, there, there_tot, do)


def backward_kernel(groups, has_dq, has_dkv, c_ref, kv0_ref, kv1_ref, *rest):
    rows, rest = rest[: 3 * groups], rest[3 * groups :]
    dq_in, rest = (rest[:groups], rest[groups:]) if has_dq else ((), rest)
    dkv_in, rest = (rest[0], rest[1:]) if has_dkv else (None, rest)
    dq_out, dkv_out = rest[:groups], rest[groups]
    dqs, dkv = rest[groups + 1 : 2 * groups + 1], rest[2 * groups + 1]
    c2 = c_ref[0, 0]
    dkv[...] = dkv_in[...] if has_dkv else jnp.zeros_like(dkv)
    for g in range(groups):
        q_ref, do_ref, stat_ref = rows[3 * g : 3 * g + 3]
        dq = dqs[g]
        dq[...] = dq_in[g][...] if has_dq else jnp.zeros_like(dq)

        size = kv0_ref.shape[0]
        for n, kv_ref in enumerate((kv0_ref, kv1_ref)):
            at = slice(n * size, (n + 1) * size)
            k = kv_ref[:, 0:128]
            p = jnp.exp2(dot(k, q_ref[...], NT) * c2 - stat_ref[0:1, :])
            t = (p * (dot(kv_ref[:, 128:256], do_ref[...], NT) - stat_ref[1:2, :])).astype(B)
            dkv[at, 128:256] += dot(p.astype(B), do_ref[...])
            dkv[at, 0:128] += dot(t, q_ref[...])
            dq[...] += dot(t, k, TN)

        dq_out[g][...] = dq[...].astype(dq_out[g].dtype)
    dkv_out[...] = dkv[...].astype(dkv_out.dtype)


def backward_block(c2, kv, rows, dq=(), dkv=(), dq_type=F, dkv_type=F):
    count, keys, groups = rows[0][0].shape[0], 2 * kv[0].shape[0], len(rows)
    vmem = pl.BlockSpec(memory_space=pltpu.VMEM)
    args = [c2, *kv, *(x for group in rows for x in group), *dq, *dkv]
    *dqs, dkv = pl.pallas_call(
        functools.partial(backward_kernel, groups, bool(dq), bool(dkv)),
        in_specs=[pl.BlockSpec(memory_space=pltpu.SMEM)] + [vmem] * (len(args) - 1),
        out_specs=[vmem] * (groups + 1),
        out_shape=[jax.ShapeDtypeStruct((count, 128), dq_type)] * groups
        + [jax.ShapeDtypeStruct((keys, 256), dkv_type)],
        scratch_shapes=[pltpu.VMEM((count, 128), F)] * groups + [pltpu.VMEM((keys, 256), F)],
        name="backward_block",
        cost_estimate=pl.CostEstimate(
            flops=10 * groups * count * keys * 128,
            bytes_accessed=count * 3072,
            transcendentals=groups * count * keys,
        ),
    )(*args)
    return dqs, dkv


def raw_kernel(c_ref, dq_ref, there_ref, dkv_ref, b0_ref, b1_ref, b2_ref, raw_ref, *rest):
    near, near_core, far, flat_out = rest
    coeff = c_ref[0, 0]

    def back(lo, hi):
        far = b0_ref[:, lo:hi].astype(F) + b1_ref[:, lo:hi].astype(F) + b2_ref[:, lo:hi].astype(F)
        return dkv_ref[:, lo:hi] + far

    dq = (dq_ref[...] + there_ref[...].astype(F)) * coeff
    grads = [
        unit_grad(dq, *unit_rows(raw_ref[:, 0:128])),
        unit_grad(back(0, 128) * coeff, *unit_rows(raw_ref[:, 128:256])),
        back(128, 256),
    ]
    for k, grad in enumerate(grads):
        at = slice(k * 128, (k + 1) * 128)
        flat_out[at, :] = grad.T.astype(B)
        by_core(grad.astype(B), near, near_core, far, at)


def finish_raw(coeff, dq, there, dkv, backs, raw):
    count = dq.shape[0]
    vmem = pl.BlockSpec(memory_space=pltpu.VMEM)
    return pl.pallas_call(
        raw_kernel,
        in_specs=[pl.BlockSpec(memory_space=pltpu.SMEM)] + [vmem] * 7,
        out_shape=[jax.ShapeDtypeStruct((count // n, 384), B) for n in (4, 4, 2)]
        + [jax.ShapeDtypeStruct((384, count), B)],
        name="finish_raw",
    )(coeff, dq, there, dkv, *backs, raw)


def embed(timestep, count):
    index = jnp.arange(count, dtype=F)
    freqs = jnp.exp(-math.log(10000.0) * index / count)
    angles = timestep.astype(F)[0] * freqs
    return jnp.concatenate([jnp.cos(angles), jnp.sin(angles)])


def unit_rows(values):
    factor = lax.rsqrt(jnp.mean(values * values, -1, keepdims=True) + epsilon)
    return (values * factor, factor)


def unit_grad(grad_unit, unit, factor):
    return factor * (grad_unit - unit * jnp.mean(grad_unit * unit, -1, keepdims=True))


def layer(tokens, timestep, mod_weight, qkv_weight, attn_scale, out_weight, grad_update):
    coeff = attn_scale[0] / 128
    c2 = (coeff * (1.0 / math.log(2.0))).reshape(1, 1)
    embedded = embed(timestep, mod_weight.shape[0] // 2)
    gain = 1.0 + jnp.sum(embedded[:, None] * mod_weight, 0)
    tok_float = tokens.astype(F)
    rstd = lax.rsqrt(jnp.mean(tok_float * tok_float, -1, keepdims=True) + epsilon)
    normed = tok_float * rstd
    hidden = (normed * gain).astype(B)

    across = col_move(hidden, xhi=1)
    slots = []
    for base in (hidden, across):
        slots.append([base] + [col_move(base, y=d) for d in TURNS])
    for n in range(2):
        slots[n] = with_core(slots[n])
    weights, outs = share_weight(qkv_weight), share_weight(out_weight)
    half_q, kv0, half_raw = project(qkv_weight, slots[0])
    own_q, kv1, raw = project(qkv_weight, slots[1], (half_q, half_raw))
    chunk = {0: [kv0, kv1]}
    for d in (1, 3, 2):
        chunk[d] = []
        for kv in (kv0, kv1):
            chunk[d].append(row_move(kv, z=d))
    q = row_move(own_q, xlo=1)

    across = col_move(grad_update, xhi=1)
    base = after(jnp.concatenate([grad_update, across], 0), kv1)
    cots = [base] + [col_move(base, y=d) for d in TURNS]
    cots = with_core(cots)
    own_do = project_cotangent(out_weight, cots)
    do = row_move(own_do, xlo=1)

    state_a = forward_block(c2, own_q, chunk[0])
    state = forward_block(c2, q, chunk[0])
    state = forward_block(c2, q, chunk[1] + chunk[3], state)
    acc, tot = forward_block(c2, q, chunk[2], state, last=True)
    there, there_tot = row_move(acc, xlo=1), row_move(tot, xlo=1)
    acc, tot = forward_block(c2, own_q, chunk[1] + chunk[3] + chunk[2], state_a)
    *att, flat_att, own_stats = finish_attended(acc, tot, there, there_tot, own_do)
    stats = row_move(own_stats, xlo=1)

    own, other = (own_q, own_do, own_stats), (q, do, stats)
    back = {}
    dq_a, dkv = backward_block(c2, chunk[2], [own])
    dq_p, dkv = backward_block(c2, chunk[2], [other], dkv=[dkv], dkv_type=B)
    back[2] = row_move(dkv, z=-2)
    dqs = dq_a + dq_p
    for d in (1, 3):
        dqs, dkv = backward_block(c2, chunk[d], [own, other], dqs, dkv_type=B)
        back[d] = row_move(dkv, z=-d)
    dq_p, dkv = backward_block(c2, chunk[0], [other], dqs[1:], dq_type=B)
    there = row_move(dq_p[0], xlo=1)
    dq_a, dkv = backward_block(c2, chunk[0], [own], dqs[:1], [dkv])

    *grads, flat = finish_raw(
        coeff.reshape(1, 1), dq_a[0], there, dkv, [back[1], back[2], back[3]], raw
    )
    grads = share_rows(*grads)
    atts = share_rows(*att)
    part = weight_grads(flat, flat_att, slots[0] + slots[1], cots)
    part = lax.all_to_all(part, "row", 0, 0, tiled=True)
    grad_hidden = to_owners(over_heads(grads, weights))
    update = to_owners(over_heads(atts, outs)).astype(B)
    total = jnp.sum(part.astype(F), 0)
    grad_qkv = jnp.transpose(total[:384].reshape(3, 128, 256), (0, 2, 1))
    grad_normed = grad_hidden * gain
    grad_tokens = (
        rstd * (grad_normed - normed * jnp.mean(grad_normed * normed, -1, keepdims=True))
    ).astype(B)
    return (update, grad_tokens, grad_qkv, total[384:])


def solution(mesh):
    placed = (
        P(("row", "col"), None),
        P(),
        P(),
        P(None, None, "col"),
        P("col"),
        P("col", None),
        P(("row", "col"), None),
    )
    return jax.shard_map(
        layer,
        mesh=mesh,
        in_specs=placed,
        out_specs=(
            P(("row", "col"), None),
            P(("row", "col"), None),
            P(None, "row", "col"),
            P("col", "row"),
        ),
        check_vma=False,
    )
```

```python
import functools
import math

import jax
import jax.numpy as jnp
from jax import lax
from jax.experimental import pallas as pl
from jax.experimental.pallas import tpu as pltpu
from jax.sharding import PartitionSpec as P


epsilon = 1e-06
F = jnp.float32
B = jnp.bfloat16
NT = (((1,), (1,)), ((), ()))
NN = (((1,), (0,)), ((), ()))
TN = (((0,), (0,)), ((), ()))


def dot(a, b, dims=NN):
    return lax.dot_general(a, b, dims, preferred_element_type=F)


def col_move(x, xhi=0, y=0, core=0):
    perm = []
    for h in range(2):
        for w in range(4):
            for k in range(2):
                perm.append((h * 8 + w * 2 + k, (h ^ xhi) * 8 + (w + y) % 4 * 2 + (k ^ core)))
    return lax.ppermute(x, "col", perm)


def row_move(x, z=0, xlo=0):
    perm = []
    for w in range(4):
        for k in range(2):
            perm.append((w * 2 + k, (w + z) % 4 * 2 + (k ^ xlo)))
    return lax.ppermute(x, "row", perm)


def after(x, *deps):
    return lax.optimization_barrier((x,) + deps)[0]


TURNS = (1, 3, 2)


def with_core(slots):
    pairs = [(slot, col_move(slot, core=1)) for slot in slots]
    return [slot for pair in pairs for slot in pair]


def project_kernel(second, w_ref, *rest):
    slots, rest = rest[:8], rest[8:]
    prev, rest = (rest[:2], rest[2:]) if second else ((), rest)
    q_out, kv_out, raw_out, rows, weight = rest
    size = slots[0].shape[0]
    base = prev[0].shape[0] if second else 0
    for n, slot in enumerate(slots):
        rows[n * size : (n + 1) * size, :] = slot[...]
    for k in range(3):
        weight[:, k * 128 : (k + 1) * 128] = w_ref[k]
    if second:
        q_out[0:base, :] = prev[0][...]
        raw_out[0:base, :] = prev[1][...]

    @pl.loop(0, 2)
    def _(n):
        raw = dot(rows[pl.ds(pl.multiple_of(n * 256, 256), 256), :], weight[...])
        at = pl.ds(pl.multiple_of(base + n * 256, 256), 256)
        here = pl.ds(pl.multiple_of(n * 256, 256), 256)
        q_out[at, :] = unit_rows(raw[:, :128])[0].astype(B)
        kv_out[here, 0:128] = unit_rows(raw[:, 128:256])[0].astype(B)
        kv_out[here, 128:256] = raw[:, 256:].astype(B)
        raw_out[at, :] = raw[:, :256]


def project(weight, slots, prev=()):
    rows, width = 8 * slots[0].shape[0], slots[0].shape[1]
    total = rows * (2 if prev else 1)
    vmem = pl.BlockSpec(memory_space=pltpu.VMEM)
    return pl.pallas_call(
        functools.partial(project_kernel, bool(prev)),
        in_specs=[vmem] * (9 + len(prev)),
        out_shape=[
            jax.ShapeDtypeStruct((total, 128), B),
            jax.ShapeDtypeStruct((rows, 256), B),
            jax.ShapeDtypeStruct((total, 256), F),
        ],
        scratch_shapes=[
            pltpu.VMEM((rows, width), B),
            pltpu.VMEM((width, 384), B),
        ],
        name="project",
        cost_estimate=pl.CostEstimate(
            flops=2 * rows * width * 384, bytes_accessed=6 * 1024 * 1024, transcendentals=0
        ),
    )(weight, *slots, *prev)


def token_copies(slots, rows, sems):
    half = slots[0].shape[0] // 2
    return [
        pltpu.make_async_copy(
            slot.at[pl.ds(h * half, half)], rows.at[pl.ds((h * 8 + n) * half, half)], sems.at[h * 8 + n]
        )
        for h in range(2)
        for n, slot in enumerate(slots)
    ]


def cotangent_kernel(w_ref, *rest):
    slots, (out_ref, rows) = rest[:8], rest[8:]
    half = slots[0].shape[0] // 2
    for h in range(2):
        for n, slot in enumerate(slots):
            rows[(h * 8 + n) * half : (h * 8 + n + 1) * half, :] = slot[h * half : (h + 1) * half, :]

    @pl.loop(0, 2)
    def _(n):
        at = pl.ds(pl.multiple_of(n * 512, 512), 512)
        out_ref[at, :] = dot(rows[at, :], w_ref[...], NT).astype(B)


def project_cotangent(weight, slots):
    rows, width = 8 * slots[0].shape[0], slots[0].shape[1]
    vmem = pl.BlockSpec(memory_space=pltpu.VMEM)
    return pl.pallas_call(
        cotangent_kernel,
        in_specs=[vmem] * 9,
        out_shape=jax.ShapeDtypeStruct((rows, 128), B),
        scratch_shapes=[pltpu.VMEM((rows, width), B)],
        name="project_cotangent",
        cost_estimate=pl.CostEstimate(
            flops=2 * rows * width * 128, bytes_accessed=5 * 1024 * 1024, transcendentals=0
        ),
    )(weight, *slots)


def weight_grad_kernel(left_ref, att_ref, *rest):
    parts, slots, (out_ref, rows, cots, sems) = rest[:16], rest[16:24], rest[24:]
    size = parts[0].shape[0]
    first = [
        pltpu.make_async_copy(part, rows.at[pl.ds(n * size, size)], sems.at[16 + n])
        for n, part in enumerate(parts)
    ]
    second = token_copies(slots, cots, sems)
    for copy in first + second:
        copy.start()
    for copy in first:
        copy.wait()

    @pl.loop(0, 8)
    def _(n):
        at = pl.ds(pl.multiple_of(n * 256, 256), 256)
        out_ref[n, 0:384, :] = dot(left_ref[...], rows[:, at]).astype(B)

    for copy in second:
        copy.wait()

    @pl.loop(0, 8)
    def _(n):
        at = pl.ds(pl.multiple_of(n * 256, 256), 256)
        out_ref[n, 384:512, :] = dot(att_ref[...], cots[:, at]).astype(B)


def weight_grads(left, att, parts, slots):
    rows, width = left.shape[1], slots[0].shape[1]
    vmem = pl.BlockSpec(memory_space=pltpu.VMEM)
    return pl.pallas_call(
        weight_grad_kernel,
        in_specs=[vmem] * 2 + [pl.BlockSpec(memory_space=pltpu.HBM)] * 24,
        out_shape=jax.ShapeDtypeStruct((8, 512, width // 8), B),
        scratch_shapes=[pltpu.VMEM((rows, width), B)] * 2 + [pltpu.SemaphoreType.DMA((32,))],
        name="weight_grads",
        cost_estimate=pl.CostEstimate(
            flops=2 * rows * width * 512, bytes_accessed=11 * 1024 * 1024, transcendentals=0
        ),
    )(left, att, *parts, *slots)


def heads_kernel(count, *rest):
    rows, weights, slots = rest[:count], rest[count : 2 * count], rest[2 * count :]
    left = jnp.concatenate([row[...] for row in rows], 1)
    if len(weights[0].shape) == 3:
        grad = dot(left, jnp.concatenate([w[n] for w in weights for n in range(3)], 1), NT)
    else:
        grad = dot(left, jnp.concatenate([w[...] for w in weights], 0))
    size = grad.shape[0] // 4
    for n, slot in enumerate(slots):
        slot[...] = grad[n * size : (n + 1) * size].astype(slot.dtype)


def over_heads(rows, weights):
    count, width = rows[-1].shape
    if len(weights[0].shape) == 3:
        cut = pl.BlockSpec((3, 512, 128), lambda i: (0, i, 0))
    else:
        cut = pl.BlockSpec((128, 512), lambda i: (0, i))
    slot = pl.BlockSpec((count // 4, 512), lambda i: (0, i))
    return pl.pallas_call(
        functools.partial(heads_kernel, len(rows)),
        grid=(4,),
        in_specs=[pl.BlockSpec((count, width), lambda i: (0, 0))] * len(rows) + [cut] * len(rows),
        out_specs=[slot] * 4,
        out_shape=[jax.ShapeDtypeStruct((count // 4, 2048), F)]
        + [jax.ShapeDtypeStruct((count // 4, 2048), B)] * 3,
        name="over_heads",
        cost_estimate=pl.CostEstimate(
            flops=2 * count * width * 4 * 2048, bytes_accessed=8 * 1024 * 1024, transcendentals=0
        ),
    )(*rows, *weights)


def share_rows(near, near_core, far):
    across = col_move(far, xhi=1)
    rest = [col_move(x, core=1) for x in (near_core, across[across.shape[0] // 2 :])]
    return [near, across] + rest


def share_weight(weight):
    across = col_move(weight, xhi=1)
    return [weight, across, col_move(weight, core=1), col_move(across, core=1)]


def to_owners(slots):
    there = [col_move(slot, y=-d) for slot, d in zip(slots[1:], TURNS)]
    return slots[0] + there[0].astype(F) + there[1].astype(F) + there[2].astype(F)


def by_core(rows, near, near_core, far, at=slice(None)):
    size = rows.shape[0] // 16
    for y in range(4):
        for k in range(2):
            piece = rows[(2 * y + k) * size : (2 * y + k + 1) * size]
            (near_core if k else near)[y * size : (y + 1) * size, at] = piece
            piece = rows[(8 + 2 * y + k) * size : (9 + 2 * y + k) * size]
            far[(4 * k + y) * size : (4 * k + y + 1) * size, at] = piece


def forward_kernel(first, last, count, c_ref, q_ref, *rest):
    kvs, rest = rest[:count], rest[count:]
    prev, rest = ((), rest) if first else (rest[:2], rest[2:])
    acc_out, tot_out, acc, tot, kv_all = rest if last else (None, None) + rest
    c2 = c_ref[0, 0]
    step = kvs[0].shape[0]
    for n, kv_ref in enumerate(kvs):
        kv_all[n * step : (n + 1) * step, :] = kv_ref[...]
    if first:
        acc[...] = jnp.zeros_like(acc)
        tot[...] = jnp.zeros_like(tot)
    else:
        acc[...] = prev[0][...]
        tot[...] = prev[1][...]

    @pl.loop(0, count // 2)
    def _(j):
        for n in range(2):
            at = pl.ds(pl.multiple_of((2 * j + n) * step, step), step)
            w = jnp.exp2(dot(q_ref[...], kv_all[at, 0:128], NT) * c2)
            part = w[:, 0:128]
            for g in range(1, step // 128):
                part = part + w[:, g * 128 : (g + 1) * 128]
            tot[...] += part
            acc[...] += dot(w.astype(B), kv_all[at, 128:256])

    if last:
        acc_out[...] = acc[...].astype(B)
        tot_out[...] = jnp.broadcast_to(jnp.sum(tot[...].T, 0, keepdims=True), tot_out.shape)


def forward_block(c2, q, kvs, state=(), last=False):
    count, keys = q.shape[0], kvs[0].shape[0]
    vmem = pl.BlockSpec(memory_space=pltpu.VMEM)
    args = [c2, q, *kvs, *state]
    scratch = [pltpu.VMEM((len(kvs) * keys, 256), B)]
    if last:
        out = [jax.ShapeDtypeStruct((count, 128), B), jax.ShapeDtypeStruct((8, count), F)]
        scratch = [pltpu.VMEM((count, 128), F)] * 2 + scratch
    else:
        out = [jax.ShapeDtypeStruct((count, 128), F)] * 2
    return pl.pallas_call(
        functools.partial(forward_kernel, not state, last, len(kvs)),
        in_specs=[pl.BlockSpec(memory_space=pltpu.SMEM)] + [vmem] * (len(args) - 1),
        out_specs=[vmem] * 2,
        out_shape=out,
        scratch_shapes=scratch,
        name="forward_block",
        cost_estimate=pl.CostEstimate(
            flops=4 * len(kvs) * count * keys * 128,
            bytes_accessed=count * 2048,
            transcendentals=len(kvs) * count * keys,
        ),
    )(*args)


def attended_kernel(acc_ref, tot_ref, there_ref, there_tot_ref, do_ref, *rest):
    near, near_core, far, flat_out, stat_out = rest
    total = jnp.sum(tot_ref[...].T, 0, keepdims=True) + there_tot_ref[0:1, :]
    divisor = jnp.broadcast_to(total, (128, total.shape[1])).T
    attended = ((acc_ref[...] + there_ref[...].astype(F)) / divisor).astype(B)
    wide = attended.astype(F)
    delta = jnp.sum((do_ref[...].astype(F) * wide).T, 0, keepdims=True)
    flat_out[...] = wide.T.astype(B)
    by_core(attended, near, near_core, far)
    stat_out[0:1, :] = jnp.log2(total)
    stat_out[1:2, :] = delta
    stat_out[2:8, :] = jnp.zeros((6, total.shape[1]), F)


def finish_attended(acc, tot, there, there_tot, do):
    count = acc.shape[0]
    return pl.pallas_call(
        attended_kernel,
        out_shape=[jax.ShapeDtypeStruct((count // n, 128), B) for n in (4, 4, 2)]
        + [jax.ShapeDtypeStruct((128, count), B), jax.ShapeDtypeStruct((8, count), F)],
        name="finish_attended",
    )(acc, tot, there, there_tot, do)


def backward_kernel(groups, has_dq, has_dkv, c_ref, kv0_ref, kv1_ref, *rest):
    rows, rest = rest[: 3 * groups], rest[3 * groups :]
    dq_in, rest = (rest[:groups], rest[groups:]) if has_dq else ((), rest)
    dkv_in, rest = (rest[0], rest[1:]) if has_dkv else (None, rest)
    dq_out, dkv_out = rest[:groups], rest[groups]
    dqs, dkv = rest[groups + 1 : 2 * groups + 1], rest[2 * groups + 1]
    c2 = c_ref[0, 0]
    dkv[...] = dkv_in[...] if has_dkv else jnp.zeros_like(dkv)
    for g in range(groups):
        q_ref, do_ref, stat_ref = rows[3 * g : 3 * g + 3]
        dq = dqs[g]
        dq[...] = dq_in[g][...] if has_dq else jnp.zeros_like(dq)

        size = kv0_ref.shape[0]
        for n, kv_ref in enumerate((kv0_ref, kv1_ref)):
            at = slice(n * size, (n + 1) * size)
            k = kv_ref[:, 0:128]
            p = jnp.exp2(dot(k, q_ref[...], NT) * c2 - stat_ref[0:1, :])
            t = (p * (dot(kv_ref[:, 128:256], do_ref[...], NT) - stat_ref[1:2, :])).astype(B)
            dkv[at, 128:256] += dot(p.astype(B), do_ref[...])
            dkv[at, 0:128] += dot(t, q_ref[...])
            dq[...] += dot(t, k, TN)

        dq_out[g][...] = dq[...].astype(dq_out[g].dtype)
    dkv_out[...] = dkv[...].astype(dkv_out.dtype)


def backward_block(c2, kv, rows, dq=(), dkv=(), dq_type=F, dkv_type=F):
    count, keys, groups = rows[0][0].shape[0], 2 * kv[0].shape[0], len(rows)
    vmem = pl.BlockSpec(memory_space=pltpu.VMEM)
    args = [c2, *kv, *(x for group in rows for x in group), *dq, *dkv]
    *dqs, dkv = pl.pallas_call(
        functools.partial(backward_kernel, groups, bool(dq), bool(dkv)),
        in_specs=[pl.BlockSpec(memory_space=pltpu.SMEM)] + [vmem] * (len(args) - 1),
        out_specs=[vmem] * (groups + 1),
        out_shape=[jax.ShapeDtypeStruct((count, 128), dq_type)] * groups
        + [jax.ShapeDtypeStruct((keys, 256), dkv_type)],
        scratch_shapes=[pltpu.VMEM((count, 128), F)] * groups + [pltpu.VMEM((keys, 256), F)],
        name="backward_block",
        cost_estimate=pl.CostEstimate(
            flops=10 * groups * count * keys * 128,
            bytes_accessed=count * 3072,
            transcendentals=groups * count * keys,
        ),
    )(*args)
    return dqs, dkv


def raw_kernel(c_ref, dq_ref, there_ref, dkv_ref, b0_ref, b1_ref, b2_ref, raw_ref, *rest):
    near, near_core, far, flat_out = rest
    coeff = c_ref[0, 0]

    def back(lo, hi):
        far = b0_ref[:, lo:hi].astype(F) + b1_ref[:, lo:hi].astype(F) + b2_ref[:, lo:hi].astype(F)
        return dkv_ref[:, lo:hi] + far

    dq = (dq_ref[...] + there_ref[...].astype(F)) * coeff
    grads = [
        unit_grad(dq, *unit_rows(raw_ref[:, 0:128])),
        unit_grad(back(0, 128) * coeff, *unit_rows(raw_ref[:, 128:256])),
        back(128, 256),
    ]
    for k, grad in enumerate(grads):
        at = slice(k * 128, (k + 1) * 128)
        flat_out[at, :] = grad.T.astype(B)
        by_core(grad.astype(B), near, near_core, far, at)


def finish_raw(coeff, dq, there, dkv, backs, raw):
    count = dq.shape[0]
    vmem = pl.BlockSpec(memory_space=pltpu.VMEM)
    return pl.pallas_call(
        raw_kernel,
        in_specs=[pl.BlockSpec(memory_space=pltpu.SMEM)] + [vmem] * 7,
        out_shape=[jax.ShapeDtypeStruct((count // n, 384), B) for n in (4, 4, 2)]
        + [jax.ShapeDtypeStruct((384, count), B)],
        name="finish_raw",
    )(coeff, dq, there, dkv, *backs, raw)


def embed(timestep, count):
    index = jnp.arange(count, dtype=F)
    freqs = jnp.exp(-math.log(10000.0) * index / count)
    angles = timestep.astype(F)[0] * freqs
    return jnp.concatenate([jnp.cos(angles), jnp.sin(angles)])


def unit_rows(values):
    factor = lax.rsqrt(jnp.mean(values * values, -1, keepdims=True) + epsilon)
    return (values * factor, factor)


def unit_grad(grad_unit, unit, factor):
    return factor * (grad_unit - unit * jnp.mean(grad_unit * unit, -1, keepdims=True))


def layer(tokens, timestep, mod_weight, qkv_weight, attn_scale, out_weight, grad_update):
    coeff = attn_scale[0] / 128
    c2 = (coeff * (1.0 / math.log(2.0))).reshape(1, 1)
    embedded = embed(timestep, mod_weight.shape[0] // 2)
    gain = 1.0 + jnp.sum(embedded[:, None] * mod_weight, 0)
    tok_float = tokens.astype(F)
    rstd = lax.rsqrt(jnp.mean(tok_float * tok_float, -1, keepdims=True) + epsilon)
    normed = tok_float * rstd
    hidden = (normed * gain).astype(B)

    across = col_move(hidden, xhi=1)
    slots = []
    for base in (hidden, across):
        slots.append([base] + [col_move(base, y=d) for d in TURNS])
    for n in range(2):
        slots[n] = with_core(slots[n])
    weights, outs = share_weight(qkv_weight), share_weight(out_weight)
    half_q, kv0, half_raw = project(qkv_weight, slots[0])
    own_q, kv1, raw = project(qkv_weight, slots[1], (half_q, half_raw))
    chunk = {0: [kv0, kv1]}
    for d in (1, 3, 2):
        chunk[d] = []
        for kv in (kv0, kv1):
            chunk[d].append(row_move(kv, z=d))
    q = row_move(own_q, xlo=1)

    across = col_move(grad_update, xhi=1)
    base = after(jnp.concatenate([grad_update, across], 0), kv1)
    cots = [base] + [col_move(base, y=d) for d in TURNS]
    cots = with_core(cots)
    own_do = project_cotangent(out_weight, cots)
    do = row_move(own_do, xlo=1)

    state = forward_block(c2, own_q, chunk[0])
    acc, tot = forward_block(c2, own_q, chunk[1] + chunk[3] + chunk[2], state)
    acc_p, tot_p = forward_block(
        c2, q, chunk[0] + chunk[1] + chunk[3] + chunk[2], last=True
    )
    there, there_tot = row_move(acc_p, xlo=1), row_move(tot_p, xlo=1)
    *att, flat_att, own_stats = finish_attended(acc, tot, there, there_tot, own_do)
    stats = row_move(own_stats, xlo=1)

    own, other = (own_q, own_do, own_stats), (q, do, stats)
    back = {}
    dq_a, dkv = backward_block(c2, chunk[2], [own])
    dq_p, dkv = backward_block(c2, chunk[2], [other], dkv=[dkv], dkv_type=B)
    back[2] = row_move(dkv, z=-2)
    dqs = dq_a + dq_p
    for d in (1, 3):
        dqs, dkv = backward_block(c2, chunk[d], [own, other], dqs, dkv_type=B)
        back[d] = row_move(dkv, z=-d)
    dq_p, dkv = backward_block(c2, chunk[0], [other], dqs[1:], dq_type=B)
    there = row_move(dq_p[0], xlo=1)
    dq_a, dkv = backward_block(c2, chunk[0], [own], dqs[:1], [dkv])

    *grads, flat = finish_raw(
        coeff.reshape(1, 1), dq_a[0], there, dkv, [back[1], back[2], back[3]], raw
    )
    grads = share_rows(*grads)
    atts = share_rows(*att)
    part = weight_grads(flat, flat_att, slots[0] + slots[1], cots)
    part = lax.all_to_all(part, "row", 0, 0, tiled=True)
    grad_hidden = to_owners(over_heads(grads, weights))
    update = to_owners(over_heads(atts, outs)).astype(B)
    total = jnp.sum(part.astype(F), 0)
    grad_qkv = jnp.transpose(total[:384].reshape(3, 128, 256), (0, 2, 1))
    grad_normed = grad_hidden * gain
    grad_tokens = (
        rstd * (grad_normed - normed * jnp.mean(grad_normed * normed, -1, keepdims=True))
    ).astype(B)
    return (update, grad_tokens, grad_qkv, total[384:])


def solution(mesh):
    placed = (
        P(("row", "col"), None),
        P(),
        P(),
        P(None, None, "col"),
        P("col"),
        P("col", None),
        P(("row", "col"), None),
    )
    return jax.shard_map(
        layer,
        mesh=mesh,
        in_specs=placed,
        out_specs=(
            P(("row", "col"), None),
            P(("row", "col"), None),
            P(None, "row", "col"),
            P("col", "row"),
        ),
        check_vma=False,
    )
```

```python
import functools
import math

import jax
import jax.numpy as jnp
from jax import lax
from jax.experimental import pallas as pl
from jax.experimental.pallas import tpu as pltpu
from jax.sharding import PartitionSpec as P


epsilon = 1e-06
F = jnp.float32
B = jnp.bfloat16
NT = (((1,), (1,)), ((), ()))
NN = (((1,), (0,)), ((), ()))
TN = (((0,), (0,)), ((), ()))


def dot(a, b, dims=NN):
    return lax.dot_general(a, b, dims, preferred_element_type=F)


def col_move(x, xhi=0, y=0, core=0):
    perm = []
    for h in range(2):
        for w in range(4):
            for k in range(2):
                perm.append((h * 8 + w * 2 + k, (h ^ xhi) * 8 + (w + y) % 4 * 2 + (k ^ core)))
    return lax.ppermute(x, "col", perm)


def row_move(x, z=0, xlo=0):
    perm = []
    for w in range(4):
        for k in range(2):
            perm.append((w * 2 + k, (w + z) % 4 * 2 + (k ^ xlo)))
    return lax.ppermute(x, "row", perm)


def after(x, *deps):
    return lax.optimization_barrier((x,) + deps)[0]


TURNS = (1, 3, 2)


def with_core(slots):
    pairs = [(slot, col_move(slot, core=1)) for slot in slots]
    return [slot for pair in pairs for slot in pair]


def project_kernel(second, w_ref, *rest):
    slots, rest = rest[:8], rest[8:]
    prev, rest = (rest[:2], rest[2:]) if second else ((), rest)
    q_out, kv_out, raw_out, rows, weight = rest
    size = slots[0].shape[0]
    base = prev[0].shape[0] if second else 0
    for n, slot in enumerate(slots):
        rows[n * size : (n + 1) * size, :] = slot[...]
    for k in range(3):
        weight[:, k * 128 : (k + 1) * 128] = w_ref[k]
    if second:
        q_out[0:base, :] = prev[0][...]
        raw_out[0:base, :] = prev[1][...]

    @pl.loop(0, 2)
    def _(n):
        raw = dot(rows[pl.ds(pl.multiple_of(n * 256, 256), 256), :], weight[...])
        at = pl.ds(pl.multiple_of(base + n * 256, 256), 256)
        here = pl.ds(pl.multiple_of(n * 256, 256), 256)
        q_out[at, :] = unit_rows(raw[:, :128])[0].astype(B)
        kv_out[here, 0:128] = unit_rows(raw[:, 128:256])[0].astype(B)
        kv_out[here, 128:256] = raw[:, 256:].astype(B)
        raw_out[at, :] = raw[:, :256]


def project(weight, slots, prev=()):
    rows, width = 8 * slots[0].shape[0], slots[0].shape[1]
    total = rows * (2 if prev else 1)
    vmem = pl.BlockSpec(memory_space=pltpu.VMEM)
    return pl.pallas_call(
        functools.partial(project_kernel, bool(prev)),
        in_specs=[vmem] * (9 + len(prev)),
        out_shape=[
            jax.ShapeDtypeStruct((total, 128), B),
            jax.ShapeDtypeStruct((rows, 256), B),
            jax.ShapeDtypeStruct((total, 256), F),
        ],
        scratch_shapes=[
            pltpu.VMEM((rows, width), B),
            pltpu.VMEM((width, 384), B),
        ],
        name="project",
        cost_estimate=pl.CostEstimate(
            flops=2 * rows * width * 384, bytes_accessed=6 * 1024 * 1024, transcendentals=0
        ),
    )(weight, *slots, *prev)


def token_copies(slots, rows, sems):
    half = slots[0].shape[0] // 2
    return [
        pltpu.make_async_copy(
            slot.at[pl.ds(h * half, half)], rows.at[pl.ds((h * 8 + n) * half, half)], sems.at[h * 8 + n]
        )
        for h in range(2)
        for n, slot in enumerate(slots)
    ]


def cotangent_kernel(w_ref, *rest):
    slots, (out_ref, rows) = rest[:8], rest[8:]
    half = slots[0].shape[0] // 2
    for h in range(2):
        for n, slot in enumerate(slots):
            rows[(h * 8 + n) * half : (h * 8 + n + 1) * half, :] = slot[h * half : (h + 1) * half, :]

    @pl.loop(0, 4)
    def _(n):
        at = pl.ds(pl.multiple_of(n * 256, 256), 256)
        out_ref[at, :] = dot(rows[at, :], w_ref[...], NT).astype(B)


def project_cotangent(weight, slots):
    rows, width = 8 * slots[0].shape[0], slots[0].shape[1]
    vmem = pl.BlockSpec(memory_space=pltpu.VMEM)
    return pl.pallas_call(
        cotangent_kernel,
        in_specs=[vmem] * 9,
        out_shape=jax.ShapeDtypeStruct((rows, 128), B),
        scratch_shapes=[pltpu.VMEM((rows, width), B)],
        name="project_cotangent",
        cost_estimate=pl.CostEstimate(
            flops=2 * rows * width * 128, bytes_accessed=5 * 1024 * 1024, transcendentals=0
        ),
    )(weight, *slots)


def weight_grad_kernel(left_ref, att_ref, *rest):
    parts, slots, (out_ref, rows, cots, sems) = rest[:16], rest[16:24], rest[24:]
    size = parts[0].shape[0]
    first = [
        pltpu.make_async_copy(part, rows.at[pl.ds(n * size, size)], sems.at[16 + n])
        for n, part in enumerate(parts)
    ]
    second = token_copies(slots, cots, sems)
    for copy in first + second:
        copy.start()
    for copy in first:
        copy.wait()

    @pl.loop(0, 8)
    def _(n):
        at = pl.ds(pl.multiple_of(n * 256, 256), 256)
        out_ref[n, 0:384, :] = dot(left_ref[...], rows[:, at]).astype(B)

    for copy in second:
        copy.wait()

    @pl.loop(0, 8)
    def _(n):
        at = pl.ds(pl.multiple_of(n * 256, 256), 256)
        out_ref[n, 384:512, :] = dot(att_ref[...], cots[:, at]).astype(B)


def weight_grads(left, att, parts, slots):
    rows, width = left.shape[1], slots[0].shape[1]
    vmem = pl.BlockSpec(memory_space=pltpu.VMEM)
    return pl.pallas_call(
        weight_grad_kernel,
        in_specs=[vmem] * 2 + [pl.BlockSpec(memory_space=pltpu.HBM)] * 24,
        out_shape=jax.ShapeDtypeStruct((8, 512, width // 8), B),
        scratch_shapes=[pltpu.VMEM((rows, width), B)] * 2 + [pltpu.SemaphoreType.DMA((32,))],
        name="weight_grads",
        cost_estimate=pl.CostEstimate(
            flops=2 * rows * width * 512, bytes_accessed=11 * 1024 * 1024, transcendentals=0
        ),
    )(left, att, *parts, *slots)


def heads_kernel(count, *rest):
    rows, weights, slots = rest[:count], rest[count : 2 * count], rest[2 * count :]
    left = jnp.concatenate([row[...] for row in rows], 1)
    if len(weights[0].shape) == 3:
        grad = dot(left, jnp.concatenate([w[n] for w in weights for n in range(3)], 1), NT)
    else:
        grad = dot(left, jnp.concatenate([w[...] for w in weights], 0))
    size = grad.shape[0] // 4
    for n, slot in enumerate(slots):
        slot[...] = grad[n * size : (n + 1) * size].astype(slot.dtype)


def over_heads(rows, weights):
    count, width = rows[-1].shape
    if len(weights[0].shape) == 3:
        cut = pl.BlockSpec((3, 512, 128), lambda i: (0, i, 0))
    else:
        cut = pl.BlockSpec((128, 512), lambda i: (0, i))
    slot = pl.BlockSpec((count // 4, 512), lambda i: (0, i))
    return pl.pallas_call(
        functools.partial(heads_kernel, len(rows)),
        grid=(4,),
        in_specs=[pl.BlockSpec((count, width), lambda i: (0, 0))] * len(rows) + [cut] * len(rows),
        out_specs=[slot] * 4,
        out_shape=[jax.ShapeDtypeStruct((count // 4, 2048), F)]
        + [jax.ShapeDtypeStruct((count // 4, 2048), B)] * 3,
        name="over_heads",
        cost_estimate=pl.CostEstimate(
            flops=2 * count * width * 4 * 2048, bytes_accessed=8 * 1024 * 1024, transcendentals=0
        ),
    )(*rows, *weights)


def share_rows(near, near_core, far):
    across = col_move(far, xhi=1)
    rest = [col_move(x, core=1) for x in (near_core, across[across.shape[0] // 2 :])]
    return [near, across] + rest


def share_weight(weight):
    across = col_move(weight, xhi=1)
    return [weight, across, col_move(weight, core=1), col_move(across, core=1)]


def to_owners(slots):
    there = [col_move(slot, y=-d) for slot, d in zip(slots[1:], TURNS)]
    return slots[0] + there[0].astype(F) + there[1].astype(F) + there[2].astype(F)


def by_core(rows, near, near_core, far, at=slice(None)):
    size = rows.shape[0] // 16
    for y in range(4):
        for k in range(2):
            piece = rows[(2 * y + k) * size : (2 * y + k + 1) * size]
            (near_core if k else near)[y * size : (y + 1) * size, at] = piece
            piece = rows[(8 + 2 * y + k) * size : (9 + 2 * y + k) * size]
            far[(4 * k + y) * size : (4 * k + y + 1) * size, at] = piece


def forward_kernel(first, last, count, c_ref, q_ref, *rest):
    kvs, rest = rest[:count], rest[count:]
    prev, rest = ((), rest) if first else (rest[:2], rest[2:])
    acc_out, tot_out, acc, tot, kv_all = rest if last else (None, None) + rest
    c2 = c_ref[0, 0]
    step = kvs[0].shape[0]
    for n, kv_ref in enumerate(kvs):
        kv_all[n * step : (n + 1) * step, :] = kv_ref[...]
    if first:
        acc[...] = jnp.zeros_like(acc)
        tot[...] = jnp.zeros_like(tot)
    else:
        acc[...] = prev[0][...]
        tot[...] = prev[1][...]

    @pl.loop(0, count)
    def _(j):
        at = pl.ds(pl.multiple_of(j * step, step), step)
        w = jnp.exp2(dot(q_ref[...], kv_all[at, 0:128], NT) * c2)
        part = w[:, 0:128]
        for g in range(1, step // 128):
            part = part + w[:, g * 128 : (g + 1) * 128]
        tot[...] += part
        acc[...] += dot(w.astype(B), kv_all[at, 128:256])

    if last:
        acc_out[...] = acc[...].astype(B)
        tot_out[...] = jnp.broadcast_to(jnp.sum(tot[...].T, 0, keepdims=True), tot_out.shape)


def forward_block(c2, q, kvs, state=(), last=False):
    count, keys = q.shape[0], kvs[0].shape[0]
    vmem = pl.BlockSpec(memory_space=pltpu.VMEM)
    args = [c2, q, *kvs, *state]
    scratch = [pltpu.VMEM((len(kvs) * keys, 256), B)]
    if last:
        out = [jax.ShapeDtypeStruct((count, 128), B), jax.ShapeDtypeStruct((8, count), F)]
        scratch = [pltpu.VMEM((count, 128), F)] * 2 + scratch
    else:
        out = [jax.ShapeDtypeStruct((count, 128), F)] * 2
    return pl.pallas_call(
        functools.partial(forward_kernel, not state, last, len(kvs)),
        in_specs=[pl.BlockSpec(memory_space=pltpu.SMEM)] + [vmem] * (len(args) - 1),
        out_specs=[vmem] * 2,
        out_shape=out,
        scratch_shapes=scratch,
        name="forward_block",
        cost_estimate=pl.CostEstimate(
            flops=4 * len(kvs) * count * keys * 128,
            bytes_accessed=count * 2048,
            transcendentals=len(kvs) * count * keys,
        ),
    )(*args)


def attended_kernel(acc_ref, tot_ref, there_ref, there_tot_ref, do_ref, *rest):
    near, near_core, far, flat_out, stat_out = rest
    total = jnp.sum(tot_ref[...].T, 0, keepdims=True) + there_tot_ref[0:1, :]
    divisor = jnp.broadcast_to(total, (128, total.shape[1])).T
    attended = ((acc_ref[...] + there_ref[...].astype(F)) / divisor).astype(B)
    wide = attended.astype(F)
    delta = jnp.sum((do_ref[...].astype(F) * wide).T, 0, keepdims=True)
    flat_out[...] = wide.T.astype(B)
    by_core(attended, near, near_core, far)
    stat_out[0:1, :] = jnp.log2(total)
    stat_out[1:2, :] = delta
    stat_out[2:8, :] = jnp.zeros((6, total.shape[1]), F)


def finish_attended(acc, tot, there, there_tot, do):
    count = acc.shape[0]
    return pl.pallas_call(
        attended_kernel,
        out_shape=[jax.ShapeDtypeStruct((count // n, 128), B) for n in (4, 4, 2)]
        + [jax.ShapeDtypeStruct((128, count), B), jax.ShapeDtypeStruct((8, count), F)],
        name="finish_attended",
    )(acc, tot, there, there_tot, do)


def backward_kernel(groups, has_dq, has_dkv, c_ref, kv0_ref, kv1_ref, *rest):
    rows, rest = rest[: 3 * groups], rest[3 * groups :]
    dq_in, rest = (rest[:groups], rest[groups:]) if has_dq else ((), rest)
    dkv_in, rest = (rest[0], rest[1:]) if has_dkv else (None, rest)
    dq_out, dkv_out = rest[:groups], rest[groups]
    dq, dkv, q_all, do_all, stat_all, kv_all = rest[groups + 1 :]
    c2 = c_ref[0, 0]
    size, count = kv0_ref.shape[0], rows[0].shape[0]
    kv_all[0:size, :] = kv0_ref[...]
    kv_all[size : 2 * size, :] = kv1_ref[...]
    for g in range(groups):
        at = slice(g * count, (g + 1) * count)
        q_all[at, :] = rows[3 * g][...]
        do_all[at, :] = rows[3 * g + 1][...]
        stat_all[g] = rows[3 * g + 2][...]
        dq[at, :] = dq_in[g][...] if has_dq else jnp.zeros((count, 128), F)
    dkv[...] = dkv_in[...] if has_dkv else jnp.zeros_like(dkv)

    step = size if groups > 1 else size // 2
    steps = 2 * size // step

    @pl.loop(0, steps * groups)
    def _(i):
        at = pl.ds(pl.multiple_of(i % steps * step, step), step)
        here = pl.ds(pl.multiple_of(i // steps * count, count), count)
        stat = stat_all[i // steps]
        k, q, do = kv_all[at, 0:128], q_all[here, :], do_all[here, :]
        p = jnp.exp2(dot(k, q, NT) * c2 - stat[0:1, :])
        t = (p * (dot(kv_all[at, 128:256], do, NT) - stat[1:2, :])).astype(B)
        dkv[at, 128:256] += dot(p.astype(B), do)
        dkv[at, 0:128] += dot(t, q)
        dq[here, :] += dot(t, k, TN)

    for g in range(groups):
        dq_out[g][...] = dq[g * count : (g + 1) * count, :].astype(dq_out[g].dtype)
    dkv_out[...] = dkv[...].astype(dkv_out.dtype)


def backward_block(c2, kv, rows, dq=(), dkv=(), dq_type=F, dkv_type=F):
    count, keys, groups = rows[0][0].shape[0], 2 * kv[0].shape[0], len(rows)
    vmem = pl.BlockSpec(memory_space=pltpu.VMEM)
    args = [c2, *kv, *(x for group in rows for x in group), *dq, *dkv]
    *dqs, dkv = pl.pallas_call(
        functools.partial(backward_kernel, groups, bool(dq), bool(dkv)),
        in_specs=[pl.BlockSpec(memory_space=pltpu.SMEM)] + [vmem] * (len(args) - 1),
        out_specs=[vmem] * (groups + 1),
        out_shape=[jax.ShapeDtypeStruct((count, 128), dq_type)] * groups
        + [jax.ShapeDtypeStruct((keys, 256), dkv_type)],
        scratch_shapes=[
            pltpu.VMEM((groups * count, 128), F),
            pltpu.VMEM((keys, 256), F),
            pltpu.VMEM((groups * count, 128), B),
            pltpu.VMEM((groups * count, 128), B),
            pltpu.VMEM((groups, 8, count), F),
            pltpu.VMEM((keys, 256), B),
        ],
        name="backward_block",
        cost_estimate=pl.CostEstimate(
            flops=10 * groups * count * keys * 128,
            bytes_accessed=count * 3072,
            transcendentals=groups * count * keys,
        ),
    )(*args)
    return dqs, dkv


def raw_kernel(c_ref, dq_ref, there_ref, dkv_ref, b0_ref, b1_ref, b2_ref, raw_ref, *rest):
    near, near_core, far, flat_out = rest
    coeff = c_ref[0, 0]
    size = near.shape[0] // 4
    for h in range(2):

        @pl.loop(0, 4)
        def _(y):
            rows = pl.ds(pl.multiple_of((4 * h + y) * 2 * size, 2 * size), 2 * size)

            def back(lo, hi):
                total = dkv_ref[rows, lo:hi]
                for ref in (b0_ref, b1_ref, b2_ref):
                    total = total + ref[rows, lo:hi].astype(F)
                return total

            dq = (dq_ref[rows, :] + there_ref[rows, :].astype(F)) * coeff
            grads = [
                unit_grad(dq, *unit_rows(raw_ref[rows, 0:128])),
                unit_grad(back(0, 128) * coeff, *unit_rows(raw_ref[rows, 128:256])),
                back(128, 256),
            ]
            first = pl.ds(pl.multiple_of(y * size, size), size)
            last = pl.ds(pl.multiple_of((4 + y) * size, size), size)
            for k, grad in enumerate(grads):
                at = slice(k * 128, (k + 1) * 128)
                flat_out[at, rows] = grad.T.astype(B)
                grad = grad.astype(B)
                (far if h else near)[first, at] = grad[0:size]
                if h:
                    far[last, at] = grad[size : 2 * size]
                else:
                    near_core[first, at] = grad[size : 2 * size]


def finish_raw(coeff, dq, there, dkv, backs, raw):
    count = dq.shape[0]
    vmem = pl.BlockSpec(memory_space=pltpu.VMEM)
    return pl.pallas_call(
        raw_kernel,
        in_specs=[pl.BlockSpec(memory_space=pltpu.SMEM)] + [vmem] * 7,
        out_shape=[jax.ShapeDtypeStruct((count // n, 384), B) for n in (4, 4, 2)]
        + [jax.ShapeDtypeStruct((384, count), B)],
        name="finish_raw",
    )(coeff, dq, there, dkv, *backs, raw)


def embed(timestep, count):
    index = jnp.arange(count, dtype=F)
    freqs = jnp.exp(-math.log(10000.0) * index / count)
    angles = timestep.astype(F)[0] * freqs
    return jnp.concatenate([jnp.cos(angles), jnp.sin(angles)])


def unit_rows(values):
    factor = lax.rsqrt(jnp.mean(values * values, -1, keepdims=True) + epsilon)
    return (values * factor, factor)


def unit_grad(grad_unit, unit, factor):
    return factor * (grad_unit - unit * jnp.mean(grad_unit * unit, -1, keepdims=True))


def layer(tokens, timestep, mod_weight, qkv_weight, attn_scale, out_weight, grad_update):
    coeff = attn_scale[0] / 128
    c2 = (coeff * (1.0 / math.log(2.0))).reshape(1, 1)
    embedded = embed(timestep, mod_weight.shape[0] // 2)
    gain = 1.0 + jnp.sum(embedded[:, None] * mod_weight, 0)
    tok_float = tokens.astype(F)
    rstd = lax.rsqrt(jnp.mean(tok_float * tok_float, -1, keepdims=True) + epsilon)
    normed = tok_float * rstd
    hidden = (normed * gain).astype(B)

    across = col_move(hidden, xhi=1)
    slots = []
    for base in (hidden, across):
        slots.append([base] + [col_move(base, y=d) for d in TURNS])
    for n in range(2):
        slots[n] = with_core(slots[n])
    weights, outs = share_weight(qkv_weight), share_weight(out_weight)
    half_q, kv0, half_raw = project(qkv_weight, slots[0])
    own_q, kv1, raw = project(qkv_weight, slots[1], (half_q, half_raw))
    chunk = {0: [kv0, kv1]}
    for d in (1, 3, 2):
        chunk[d] = []
        for kv in (kv0, kv1):
            chunk[d].append(row_move(kv, z=d))
    q = row_move(own_q, xlo=1)

    across = col_move(grad_update, xhi=1)
    base = after(jnp.concatenate([grad_update, across], 0), kv1)
    cots = [base] + [col_move(base, y=d) for d in TURNS]
    cots = with_core(cots)
    own_do = project_cotangent(out_weight, cots)
    do = row_move(own_do, xlo=1)

    state = forward_block(c2, own_q, chunk[0])
    acc, tot = forward_block(c2, own_q, chunk[1] + chunk[3] + chunk[2], state)
    acc_p, tot_p = forward_block(
        c2, q, chunk[0] + chunk[1] + chunk[3] + chunk[2], last=True
    )
    there, there_tot = row_move(acc_p, xlo=1), row_move(tot_p, xlo=1)
    *att, flat_att, own_stats = finish_attended(acc, tot, there, there_tot, own_do)
    stats = row_move(own_stats, xlo=1)

    own, other = (own_q, own_do, own_stats), (q, do, stats)
    back = {}
    dq_a, dkv = backward_block(c2, chunk[2], [own])
    dq_p, dkv = backward_block(c2, chunk[2], [other], dkv=[dkv], dkv_type=B)
    back[2] = row_move(dkv, z=-2)
    dqs = dq_a + dq_p
    for d in (1, 3):
        dqs, dkv = backward_block(c2, chunk[d], [own, other], dqs, dkv_type=B)
        back[d] = row_move(dkv, z=-d)
    dq_p, dkv = backward_block(c2, chunk[0], [other], dqs[1:], dq_type=B)
    there = row_move(dq_p[0], xlo=1)
    dq_a, dkv = backward_block(c2, chunk[0], [own], dqs[:1], [dkv])

    *grads, flat = finish_raw(
        coeff.reshape(1, 1), dq_a[0], there, dkv, [back[1], back[2], back[3]], raw
    )
    grads = share_rows(*grads)
    atts = share_rows(*att)
    part = weight_grads(flat, flat_att, slots[0] + slots[1], cots)
    part = lax.all_to_all(part, "row", 0, 0, tiled=True)
    grad_hidden = to_owners(over_heads(grads, weights))
    update = to_owners(over_heads(atts, outs)).astype(B)
    total = jnp.sum(part.astype(F), 0)
    grad_qkv = jnp.transpose(total[:384].reshape(3, 128, 256), (0, 2, 1))
    grad_normed = grad_hidden * gain
    grad_tokens = (
        rstd * (grad_normed - normed * jnp.mean(grad_normed * normed, -1, keepdims=True))
    ).astype(B)
    return (update, grad_tokens, grad_qkv, total[384:])


def solution(mesh):
    placed = (
        P(("row", "col"), None),
        P(),
        P(),
        P(None, None, "col"),
        P("col"),
        P("col", None),
        P(("row", "col"), None),
    )
    return jax.shard_map(
        layer,
        mesh=mesh,
        in_specs=placed,
        out_specs=(
            P(("row", "col"), None),
            P(("row", "col"), None),
            P(None, "row", "col"),
            P("col", "row"),
        ),
        check_vma=False,
    )
```
